32 devices in a mesh: seq: 8 (over z, y), tp: 4 (over x, core).
Axes of the slice: x: 2, y: 2, z: 4, core: 2. Of those that a mesh axis runs over, the one named last changes fastest.
Arguments:
- states: bfloat16 [2048, 1536], P('seq', 'tp')
- modulation: float32 [3, 1536], replicated, may hold values from -2.5 to 2.5
- query_weight: bfloat16 [1536, 1536], P(None, 'tp')
- key_weight: bfloat16 [1536, 1536], P(None, 'tp')
- value_weight: bfloat16 [1536, 1536], P(None, 'tp'), may hold values from -0.15625 to 0.15625
- out_weight: bfloat16 [1536, 1536], P(None, 'tp'), may hold values from -0.15625 to 0.15625
- pattern: int32 [16, 7], replicated, may hold values from 0 to 15, as said below
Outputs:
- updated: bfloat16 [2048, 1536], P('seq', 'tp')
The draws below stay inside these ranges and needn't reach their ends.
Inputs may be any that keep to these rules, and one draw needn't show every extreme that they name: `pattern`: the 2 query tiles 2 d to 2 d + 1 list the same set of 7 distinct tiles, each in an order of its own: all tiles 2 d to 2 d + 1, and exactly one tile from each of 5 other groups of 2 tiles (group e being tiles 2 e to 2 e + 1).
All inputs are finite; a program needn't handle non-finite values.
Results may differ from the reference program's by a relative error of at most 0.0056.
Values may be sent and summed in bfloat16 or wider, within the bound.
A program may use at most 128 MiB of HBM per device.

```python
import math
import jax
import jax.numpy as jnp
from jax import lax

D = 1536
HEADS = 12
HD = 128
TILE = 128
TOKENS = 2048
TPD = 2
QTILES = 16
RSHARDS = 5
KT = 7


def draw_states(key, part):
    first = jax.random.fold_in(key, 1)
    result = jax.random.normal(first, (TOKENS, D), jnp.float32)
    return result.astype(jnp.bfloat16)


def weight_pair(key):
    base = jax.random.normal(jax.random.fold_in(key, 101), (D, D), jnp.float32) * D ** (-0.5)
    other = jax.random.normal(jax.random.fold_in(key, 102), (D, D), jnp.float32) * D ** (-0.5)
    ranks = jax.random.permutation(jax.random.fold_in(key, 103), HEADS).astype(jnp.float32)
    top_gain = 2.5
    head_gain = jnp.exp(math.log(top_gain) * ranks / (HEADS - 1))
    column_gain = jnp.repeat(head_gain, HD)[None, :]
    first_weight = base * column_gain
    second_weight = other * column_gain
    return (first_weight, second_weight)


def draw_query_weight(key, part):
    return weight_pair(key)[0].astype(jnp.bfloat16)


def draw_key_weight(key, part):
    return weight_pair(key)[1].astype(jnp.bfloat16)


def draw_pattern(key, part):
    devices = QTILES // TPD

    def one_device(device):
        device_key = jax.random.fold_in(key, device)
        order = jax.random.permutation(jax.random.fold_in(device_key, 1), devices - 1)[:RSHARDS].astype(jnp.int32)
        shard = order + (order >= device).astype(jnp.int32)
        picked = jax.random.randint(jax.random.fold_in(device_key, 2), (RSHARDS,), 0, TPD, dtype=jnp.int32)
        remote = shard * TPD + picked
        owned = device * TPD + jnp.arange(TPD, dtype=jnp.int32)
        listed = jnp.concatenate([owned, remote])

        def per_tile(tile):
            return jax.random.permutation(jax.random.fold_in(device_key, 10 + tile), listed)
        return jax.vmap(per_tile)(jnp.arange(TPD, dtype=jnp.int32))
    lists = jax.vmap(one_device)(jnp.arange(devices, dtype=jnp.int32))
    return lists.reshape(QTILES, KT).astype(jnp.int32)


def block_scale(rng, extent, cuts, smallest, largest):
    factor_of, own = 1.0, jax.random.fold_in(rng, 6)
    for axis_at, shards_of in cuts:
        steps = jnp.exp(jax.random.uniform(jax.random.fold_in(own, axis_at), (shards_of,), jnp.float32, smallest / len(cuts), largest / len(cuts)))
        factor_of = factor_of * jnp.repeat(steps, extent[axis_at] // shards_of).reshape([-1 if axis == axis_at else 1 for axis in range(len(extent))])
    return factor_of


def scatter_about(stream_key, extent, width, bound, shards=(), kind=jnp.bfloat16):
    array = jax.random.normal(stream_key, extent, jnp.float32) * width
    if len(shards) > 0:
        array = block_scale(stream_key, extent, shards, -0.22, 0.18) * array
    return jnp.clip(array, min=-bound, max=bound).astype(kind)


def setup_inputs(seed: int = 0) -> dict:
    key_of = jax.random.split(jax.random.key(seed), 8)
    states = draw_states(jax.random.fold_in(key_of[7], 71), 0)
    modulation = scatter_about(key_of[1], (3, D), 0.5, 2.5, (), jnp.float32)
    query_weight = draw_query_weight(jax.random.fold_in(key_of[7], 71), 0)
    key_weight = draw_key_weight(jax.random.fold_in(key_of[7], 71), 0)
    value_weight = scatter_about(key_of[4], (D, D), D ** -0.5, 0.15625, ((1, 4),))
    out_weight = scatter_about(key_of[5], (D, D), D ** -0.5, 0.15625, ((1, 4),))
    pattern = draw_pattern(jax.random.fold_in(key_of[7], 71), 0)
    return {"states": states, "modulation": modulation, "query_weight": query_weight, "key_weight": key_weight, "value_weight": value_weight, "out_weight": out_weight, "pattern": pattern}


def reference(states, modulation, query_weight, key_weight, value_weight, out_weight, pattern):
    states_f = states.astype(jnp.float32)
    row_mean = lax.optimization_barrier(jnp.mean(states_f, axis=1, keepdims=True))
    centered = states_f - row_mean
    variance = lax.optimization_barrier(jnp.mean(centered * centered, axis=1, keepdims=True))
    normed = (centered * lax.rsqrt(variance + 1e-06) * (1.0 + modulation[1]) + modulation[0]).astype(jnp.bfloat16)
    query = jnp.dot(normed, query_weight, preferred_element_type=jnp.float32).astype(jnp.bfloat16)
    keys = jnp.dot(normed, key_weight, preferred_element_type=jnp.float32).astype(jnp.bfloat16)
    values = jnp.dot(normed, value_weight, preferred_element_type=jnp.float32).astype(jnp.bfloat16)
    query_tiles = query.reshape(QTILES, TILE, HEADS, HD)
    key_tiles = keys.reshape(QTILES, TILE, HEADS, HD)
    value_tiles = values.reshape(QTILES, TILE, HEADS, HD)
    factor = 1.0 / math.sqrt(HD)

    def one_tile(inputs):
        query_tile, listed = inputs
        listed = listed.astype(jnp.int32)
        key_rows = jnp.take(key_tiles, listed, axis=0).reshape(KT * TILE, HEADS, HD)
        value_rows = jnp.take(value_tiles, listed, axis=0).reshape(KT * TILE, HEADS, HD)
        scores = jnp.einsum('qhd,khd->hqk', query_tile.astype(jnp.float32), key_rows.astype(jnp.float32)) * factor
        row_max = lax.optimization_barrier(jnp.max(scores, axis=2, keepdims=True))
        weights_full = jnp.exp(scores - row_max)
        weight_sum = lax.optimization_barrier(jnp.sum(weights_full, axis=2))
        weights = weights_full.astype(jnp.bfloat16)
        summed = jnp.einsum('hqk,khd->qhd', weights.astype(jnp.float32), value_rows.astype(jnp.float32))
        return (summed / jnp.transpose(weight_sum)[:, :, None]).astype(jnp.bfloat16)
    attended = lax.map(one_tile, (query_tiles, pattern)).reshape(TOKENS, D)
    projected = jnp.dot(attended, out_weight, preferred_element_type=jnp.float32)
    return (states_f + modulation[2] * projected).astype(jnp.bfloat16)
```

```python
import math

import jax
import jax.numpy as jnp
from jax import lax
from jax.experimental import pallas as pl
from jax.experimental.pallas import tpu as pltpu
from jax.sharding import PartitionSpec as P

HD = 128
TILE = 128
MESH = pl.DeviceIdType.MESH
F32 = jnp.float32
BF16 = jnp.bfloat16


def fused_kernel(
    pat, x_ref, mod, wq_hbm, wk_hbm, wv_hbm, wo_hbm, o_ref,
    zb, ys, yr, gat, att, wq, wk, wv, wo, nb, qb, kb, vb, sc,
    wsem, zup, zdn, zfw, zrv, ysn, yrv, xsn, xrv, csn, crv, dsn, drv,
    axs, axr, acs, acr, ads, adr,
):
    seq, tp = lax.axis_index("seq"), lax.axis_index("tp")
    z, y = seq // 2, seq % 2
    xx, c = tp // 2, tp % 2
    half = z // 2
    zz = z + half * (3 - 2 * z)
    step = 1 - 2 * half
    up = ((z + step) * 2 + y, tp)
    down = ((z - step) * 2 + y, tp)
    yp = (z * 2 + 1 - y, tp)
    tx = (1 - xx) * 2 + c
    tc = xx * 2 + 1 - c
    td = (1 - xx) * 2 + 1 - c
    xp = (seq, tx)
    cp = (seq, tc)
    cols = x_ref.shape[1]
    inner = zz == 1

    def remote(src, dst, ss, rs, dev):
        return pltpu.make_async_remote_copy(
            src_ref=src, dst_ref=dst, send_sem=ss, recv_sem=rs, device_id=dev, device_id_type=MESH
        )

    loads = [
        pltpu.make_async_copy(a, b, wsem.at[i])
        for i, (a, b) in enumerate(((wq_hbm, wq), (wk_hbm, wk), (wv_hbm, wv), (wo_hbm, wo)))
    ]
    for cpy in loads:
        cpy.start()

    barrier = pltpu.get_barrier_semaphore()
    for dev in (up, yp, xp, cp):
        pl.semaphore_signal(barrier, inc=1, device_id=dev, device_id_type=MESH)

    @pl.when(inner)
    def _():
        pl.semaphore_signal(barrier, inc=1, device_id=down, device_id_type=MESH)

    pl.semaphore_wait(barrier, 4 + zz)

    def own(t):
        return x_ref.at[pl.ds(t * TILE, TILE)]

    def z_own_up(t):
        return remote(own(t), zb.at[zz, t], zup.at[t], zrv.at[zz * 2 + t], up)

    def z_own_down(t):
        return remote(own(t), zb.at[0, t], zdn.at[t], zrv.at[t], down)

    def z_forward(i, t):
        if i == 0:
            return remote(zb.at[0, t], zb.at[2, t], zfw.at[t], zrv.at[4 + t], up)
        return remote(zb.at[i, t], zb.at[i, t], zfw.at[i * 2 + t], zrv.at[i * 2 + t], down)

    def z_arrive(i, t):
        remote(zb.at[i, t], zb.at[i, t], zfw.at[i * 2 + t], zrv.at[i * 2 + t], up).wait_recv()

        @pl.when(inner)
        def _():
            z_forward(i, t).start()

    def y_copy(i):
        return remote(ys.at[i], yr.at[i], ysn.at[i], yrv.at[i], yp)

    def x_copy(k):
        src = own(k) if k < 2 else gat.at[tp, k]
        return remote(src, gat.at[tp, k], xsn.at[k], xrv.at[k], xp)

    def c_copy(k):
        src = own(k) if k < 2 else gat.at[tp, k]
        return remote(src, gat.at[tp, k], csn.at[k], crv.at[k], cp)

    def d_copy(k):
        return remote(gat.at[tx, k], gat.at[tx, k], dsn.at[k], drv.at[k], cp)

    def x_arrive(k):
        remote(gat.at[tx, k], gat.at[tx, k], xsn.at[k], xrv.at[k], xp).wait_recv()
        d_copy(k).start()

    def rest_arrive(k):
        remote(gat.at[tc, k], gat.at[tc, k], csn.at[k], crv.at[k], cp).wait_recv()
        remote(gat.at[td, k], gat.at[td, k], dsn.at[k], drv.at[k], cp).wait_recv()

    for t in range(2):
        z_own_up(t).start()

        @pl.when(inner)
        def _():
            z_own_down(t).start()

        x_copy(t).start()
        c_copy(t).start()

    def place(i):
        at = (z, 1 - zz, 2, 3)[i]
        return at if i == 0 else at + half * (3 - 2 * at)

    lists = pat.shape[1]
    mine = [pat[2 * seq, n] for n in range(lists)]
    theirs = [pat[2 * (z * 2 + 1 - y), n] for n in range(lists)]

    def count(entries, value):
        return sum(jnp.where(e == value, 1, 0) for e in entries)

    def y_stage(i):
        odd = count(theirs, 2 * (place(i) * 2 + y) + 1)
        if i == 0:
            first, second = x_ref[0:TILE], x_ref[TILE:]
        else:
            first, second = zb[i - 1, 0], zb[i - 1, 1]
        ys[i] = lax.select(odd == 1, second, first)
        y_copy(i).start()

    cands = []
    rank = 0
    for i in range(4):
        for from_y in ((True,) if i == 0 else (False, True)):
            group = place(i) * 2 + ((1 - y) if from_y else y)
            even, odd = count(mine, 2 * group), count(mine, 2 * group + 1)
            cands.append((i, from_y, even, odd, rank))
            rank = rank + even + odd

    def slot_stage(k):
        value = None
        for j in range(k, k + 3):
            i, from_y, even, odd, place_of = cands[j]
            if from_y:
                options = [(even + odd, yr[i])]
            else:
                options = [(even, zb[i - 1, 0]), (odd, zb[i - 1, 1])]
            for listed, tile in options:
                if value is None:
                    value = tile
                else:
                    here = jnp.where(place_of == k, listed, 0)
                    value = lax.select(here == 1, tile, value)
        gat[tp, 2 + k] = value
        x_copy(2 + k).start()
        c_copy(2 + k).start()

    def normalize(k, row):
        blocks = [gat[t, k].astype(F32) for t in range(4)]
        width = 4 * cols
        mean = sum(jnp.sum(b, axis=1, keepdims=True) for b in blocks) / width
        blocks = [b - mean for b in blocks]
        var = sum(jnp.sum(b * b, axis=1, keepdims=True) for b in blocks) / width
        scale = lax.rsqrt(var + 1e-06)
        for t in range(4):
            lanes = slice(t * cols, (t + 1) * cols)
            nb[row : row + TILE, lanes] = (
                blocks[t] * scale * (1.0 + mod[1:2, lanes]) + mod[0:1, lanes]
            ).astype(BF16)

    heads = cols // HD
    factor = 1.0 / math.sqrt(HD)

    def project(first, rows):
        normed = nb[0:rows]
        at = first * TILE
        kb[at : at + rows] = jnp.dot(normed, wk[...], preferred_element_type=F32).astype(BF16)
        for h in range(heads):
            lanes = slice(h * HD, (h + 1) * HD)
            sc[h, :, at : at + rows] = (
                lax.dot_general(
                    qb[:, lanes], kb[at : at + rows, lanes], (((1,), (1,)), ((), ())),
                    preferred_element_type=F32,
                )
                * factor
            )
        vb[at : at + rows] = jnp.dot(normed, wv[...], preferred_element_type=F32).astype(BF16)

    def attend(k):
        rest_arrive(k)
        normalize(k, 0)
        project(k, TILE)

    y_stage(0)
    for t in range(2):
        z_arrive(0, t)
        gat[tp, t] = x_ref[t * TILE : (t + 1) * TILE]
        x_arrive(t)
    y_stage(1)
    for t in range(2):
        rest_arrive(t)
        normalize(t, t * TILE)
    for cpy in loads[:3]:
        cpy.wait()
    qb[...] = jnp.dot(nb[...], wq[...], preferred_element_type=F32).astype(BF16)
    project(0, 2 * TILE)

    def y_arrive(i):
        y_copy(i).wait_recv()

    y_arrive(0)
    y_arrive(1)
    slot_stage(0)
    z_arrive(1, 0)
    z_arrive(1, 1)
    y_stage(2)
    slot_stage(1)
    x_arrive(2)
    z_arrive(2, 0)
    x_arrive(3)
    z_arrive(2, 1)
    y_stage(3)
    y_arrive(2)
    slot_stage(2)
    slot_stage(3)
    attend(2)
    y_arrive(3)
    slot_stage(4)
    x_arrive(4)
    attend(3)
    x_arrive(5)
    attend(4)
    x_arrive(6)
    attend(5)
    attend(6)

    def att_part(t, h):
        return att.at[t, :, pl.ds(h * HD, HD)]

    def ax_copy(h):
        return remote(att_part(tp, h), att_part(tp, h), axs.at[h], axr.at[h], xp)

    def ac_copy(h):
        return remote(att_part(tp, h), att_part(tp, h), acs.at[h], acr.at[h], cp)

    def ad_copy(h):
        return remote(att_part(tx, h), att_part(tx, h), ads.at[h], adr.at[h], cp)

    for h in range(heads):
        lanes = slice(h * HD, (h + 1) * HD)
        scores = sc[h]
        full = jnp.exp(scores - jnp.max(scores, axis=1, keepdims=True))
        total = jnp.sum(full, axis=1, keepdims=True)
        summed = jnp.dot(full.astype(BF16), vb[:, lanes], preferred_element_type=F32)
        att[tp, :, lanes] = (summed / total).astype(BF16)
        ax_copy(h).start()
        ac_copy(h).start()

    loads[3].wait()
    acc = jnp.dot(att[tp], wo[tp], preferred_element_type=F32)
    for h in range(heads):
        remote(att_part(tx, h), att_part(tx, h), axs.at[h], axr.at[h], xp).wait_recv()
        ad_copy(h).start()
    for h in range(heads):
        remote(att_part(tc, h), att_part(tc, h), acs.at[h], acr.at[h], cp).wait_recv()
    acc = acc + jnp.dot(att[tc], wo[tc], preferred_element_type=F32)
    acc = acc + jnp.dot(att[tx], wo[tx], preferred_element_type=F32)
    for h in range(heads):
        remote(att_part(td, h), att_part(td, h), ads.at[h], adr.at[h], cp).wait_recv()
    acc = acc + jnp.dot(att[td], wo[td], preferred_element_type=F32)
    gate = mod[2:3, pl.ds(pl.multiple_of(tp * cols, HD), cols)]
    o_ref[...] = (x_ref[...].astype(F32) + gate * acc).astype(BF16)

    for t in range(2):
        z_own_up(t).wait_send()

        @pl.when(inner)
        def _():
            z_own_down(t).wait_send()
            for i in range(3):
                z_forward(i, t).wait_send()

    for i in range(4):
        y_copy(i).wait_send()
    for k in range(lists):
        x_copy(k).wait_send()
        c_copy(k).wait_send()
        d_copy(k).wait_send()
    for h in range(heads):
        ax_copy(h).wait_send()
        ac_copy(h).wait_send()
        ad_copy(h).wait_send()


def fused(states, modulation, query_weight, key_weight, value_weight, out_weight, pattern):
    rows, cols = states.shape
    width = modulation.shape[1]
    lists = pattern.shape[1]
    heads = cols // HD
    vmem = pl.BlockSpec(memory_space=pltpu.VMEM)
    hbm = pl.BlockSpec(memory_space=pl.ANY)
    dma = pltpu.SemaphoreType.DMA
    return pl.pallas_call(
        fused_kernel,
        out_shape=jax.ShapeDtypeStruct((rows, cols), BF16),
        in_specs=[pl.BlockSpec(memory_space=pltpu.SMEM), vmem, vmem, hbm, hbm, hbm, hbm],
        out_specs=vmem,
        scratch_shapes=[
            pltpu.VMEM((3, 2, TILE, cols), BF16),
            pltpu.VMEM((4, TILE, cols), BF16),
            pltpu.VMEM((4, TILE, cols), BF16),
            pltpu.VMEM((4, lists, TILE, cols), BF16),
            pltpu.VMEM((4, rows, cols), BF16),
            pltpu.VMEM((width, cols), BF16),
            pltpu.VMEM((width, cols), BF16),
            pltpu.VMEM((width, cols), BF16),
            pltpu.VMEM((4, cols, cols), BF16),
            pltpu.VMEM((rows, width), BF16),
            pltpu.VMEM((rows, cols), BF16),
            pltpu.VMEM((lists * TILE, cols), BF16),
            pltpu.VMEM((lists * TILE, cols), BF16),
            pltpu.VMEM((heads, rows, lists * TILE), F32),
            dma((4,)),
            dma((2,)), dma((2,)), dma((6,)), dma((6,)),
            dma((4,)), dma((4,)),
            dma((lists,)), dma((lists,)), dma((lists,)), dma((lists,)), dma((lists,)), dma((lists,)),
            dma((heads,)), dma((heads,)), dma((heads,)), dma((heads,)), dma((heads,)), dma((heads,)),
        ],
        compiler_params=pltpu.CompilerParams(
            collective_id=0, has_side_effects=True, vmem_limit_bytes=32 << 20
        ),
    )(
        pattern, states, modulation, query_weight, key_weight, value_weight,
        out_weight.reshape(4, cols, cols),
    )


def local(states, modulation, query_weight, key_weight, value_weight, out_weight, pattern):
    tok_rows, local_cols = states.shape
    col_start = lax.axis_index("tp") * local_cols
    mod_cols = lax.dynamic_slice_in_dim(modulation, col_start, local_cols, 1)
    states_f = states.astype(jnp.float32)
    gathered = lax.all_gather(states, "tp", axis=1, tiled=True)
    gathered_f = gathered.astype(jnp.float32)
    row_mean = jnp.mean(gathered_f, axis=1, keepdims=True)
    centered = gathered_f - row_mean
    variance = jnp.mean(centered * centered, axis=1, keepdims=True)
    normed = (
        centered * lax.rsqrt(variance + 1e-06) * (1.0 + modulation[1]) + modulation[0]
    ).astype(jnp.bfloat16)
    query = jnp.dot(normed, query_weight, preferred_element_type=jnp.float32).astype(jnp.bfloat16)
    keys = jnp.dot(normed, key_weight, preferred_element_type=jnp.float32).astype(jnp.bfloat16)
    values = jnp.dot(normed, value_weight, preferred_element_type=jnp.float32).astype(jnp.bfloat16)
    head_cols = query.shape[1]
    heads_local = head_cols // HD
    key_value = jnp.concatenate([keys, values], axis=1)
    tiles_dev = tok_rows // TILE
    devices = lax.axis_size("seq")
    seq_index = lax.axis_index("seq")
    list_count = pattern.shape[1]
    groups = pattern.reshape(devices, tiles_dev, list_count)
    first_lists = groups[:, 0, :]
    my_list = lax.dynamic_index_in_dim(first_lists, seq_index, 0, keepdims=False)
    all_tiles = lax.all_gather(key_value, "seq", axis=0, tiled=True)
    tile_store = all_tiles.reshape(devices * tiles_dev, TILE, 2 * head_cols)
    listed_rows = jnp.take(tile_store, my_list, axis=0).reshape(
        list_count * TILE, 2, heads_local, HD
    )
    key_rows = listed_rows[:, 0]
    value_rows = listed_rows[:, 1]
    factor = 1.0 / math.sqrt(HD)
    block_rows = min(512, tok_rows)
    block_count = tok_rows // block_rows

    def attend(query_block):
        scores = (
            jnp.einsum("qhd,khd->hqk", query_block, key_rows, preferred_element_type=jnp.float32)
            * factor
        )
        row_max = jnp.max(scores, axis=2, keepdims=True)
        weights_full = jnp.exp(scores - row_max)
        weight_sum = jnp.sum(weights_full, axis=2)
        weights = weights_full.astype(jnp.bfloat16)
        summed = jnp.einsum("hqk,khd->qhd", weights, value_rows, preferred_element_type=jnp.float32)
        return (summed / jnp.transpose(weight_sum)[:, :, None]).astype(jnp.bfloat16)

    query_blocks = query.reshape(block_count, block_rows, heads_local, HD)
    attended = lax.map(attend, query_blocks).reshape(tok_rows, head_cols)
    projected = jnp.dot(
        lax.all_gather(attended, "tp", axis=1, tiled=True),
        out_weight,
        preferred_element_type=jnp.float32,
    )
    return (states_f + mod_cols[2] * projected).astype(jnp.bfloat16)


def solution(mesh):
    placed = (P("seq", "tp"), P(), P(None, "tp"), P(None, "tp"), P(None, "tp"), P(None, "tp"), P())
    small = mesh.shape["seq"] == 8 and mesh.shape["tp"] == 4
    return jax.shard_map(
        fused if small else local, mesh=mesh, in_specs=placed, out_specs=P("seq", "tp"), check_vma=False
    )
```

```python
import math

import jax
import jax.numpy as jnp
from jax import lax
from jax.experimental import pallas as pl
from jax.experimental.pallas import tpu as pltpu
from jax.sharding import PartitionSpec as P

HD = 128
TILE = 128
MESH = pl.DeviceIdType.MESH
F32 = jnp.float32
BF16 = jnp.bfloat16


def fused_kernel(
    pat_hbm, x_hbm, mod_hbm, wq_hbm, wk_hbm, wv_hbm, wo_hbm, o_ref,
    zb, ys, yr, gat, att, wq, wk, wv, wo, nb, qb, kb, vb, sc, acc_ref, pat, x_ref, mod,
    wsem, zup, zdn, zfw, zrv, ysn, yrv, xsn, xrv, csn, crv, dsn, drv,
    axs, axr, acs, acr, ads, adr,
):
    seq, tp = lax.axis_index("seq"), lax.axis_index("tp")
    z, y = seq // 2, seq % 2
    xx, c = tp // 2, tp % 2
    half = z // 2
    zz = z + half * (3 - 2 * z)
    step = 1 - 2 * half
    up = ((z + step) * 2 + y, tp)
    down = ((z - step) * 2 + y, tp)
    yp = (z * 2 + 1 - y, tp)
    tx = (1 - xx) * 2 + c
    tc = xx * 2 + 1 - c
    td = (1 - xx) * 2 + 1 - c
    xp = (seq, tx)
    cp = (seq, tc)
    cols = x_ref.shape[1]
    inner = zz == 1

    def remote(src, dst, ss, rs, dev):
        return pltpu.make_async_remote_copy(
            src_ref=src, dst_ref=dst, send_sem=ss, recv_sem=rs, device_id=dev, device_id_type=MESH
        )

    loads = [
        pltpu.make_async_copy(a, b, wsem.at[i])
        for i, (a, b) in enumerate(((wq_hbm, wq), (wk_hbm, wk), (wv_hbm, wv), (wo_hbm, wo), (pat_hbm, pat), (x_hbm, x_ref), (mod_hbm, mod)))
    ]
    for cpy in (loads[5], loads[4], loads[6], *loads[:4]):
        cpy.start()

    barrier = pltpu.get_barrier_semaphore()
    for dev in (up, yp, xp, cp):
        pl.semaphore_signal(barrier, inc=1, device_id=dev, device_id_type=MESH)

    @pl.when(inner)
    def _():
        pl.semaphore_signal(barrier, inc=1, device_id=down, device_id_type=MESH)

    loads[5].wait()
    pl.semaphore_wait(barrier, 4 + zz)

    def own(t):
        return x_ref.at[pl.ds(t * TILE, TILE)]

    def z_own_up(t):
        return remote(own(t), zb.at[zz, t], zup.at[t], zrv.at[zz * 2 + t], up)

    def z_own_down(t):
        return remote(own(t), zb.at[0, t], zdn.at[t], zrv.at[t], down)

    def z_forward(i, t):
        if i == 0:
            return remote(zb.at[0, t], zb.at[2, t], zfw.at[t], zrv.at[4 + t], up)
        return remote(zb.at[i, t], zb.at[i, t], zfw.at[i * 2 + t], zrv.at[i * 2 + t], down)

    def z_arrive(i, t):
        remote(zb.at[i, t], zb.at[i, t], zfw.at[i * 2 + t], zrv.at[i * 2 + t], up).wait_recv()

        @pl.when(inner)
        def _():
            z_forward(i, t).start()

    def y_copy(i):
        return remote(ys.at[i], yr.at[i], ysn.at[i], yrv.at[i], yp)

    def x_copy(k):
        src = own(k) if k < 2 else gat.at[tp, k]
        return remote(src, gat.at[tp, k], xsn.at[k], xrv.at[k], xp)

    def c_copy(k):
        src = own(k) if k < 2 else gat.at[tp, k]
        return remote(src, gat.at[tp, k], csn.at[k], crv.at[k], cp)

    def d_copy(k):
        return remote(gat.at[tx, k], gat.at[tx, k], dsn.at[k], drv.at[k], cp)

    def x_arrive(k):
        remote(gat.at[tx, k], gat.at[tx, k], xsn.at[k], xrv.at[k], xp).wait_recv()
        d_copy(k).start()

    def rest_arrive(k):
        remote(gat.at[tc, k], gat.at[tc, k], csn.at[k], crv.at[k], cp).wait_recv()
        remote(gat.at[td, k], gat.at[td, k], dsn.at[k], drv.at[k], cp).wait_recv()

    for t in range(2):
        z_own_up(t).start()

        @pl.when(inner)
        def _():
            z_own_down(t).start()

        x_copy(t).start()
        c_copy(t).start()

    def place(i):
        at = (z, 1 - zz, 2, 3)[i]
        return at if i == 0 else at + half * (3 - 2 * at)

    loads[4].wait()
    lists = pat.shape[0]
    mine = [pat[n, 2 * seq] for n in range(lists)]
    theirs = [pat[n, 2 * (z * 2 + 1 - y)] for n in range(lists)]

    def count(entries, value):
        return sum(jnp.where(e == value, 1, 0) for e in entries)

    def y_stage(i):
        odd = count(theirs, 2 * (place(i) * 2 + y) + 1)
        if i == 0:
            first, second = x_ref[0:TILE], x_ref[TILE:]
        else:
            first, second = zb[i - 1, 0], zb[i - 1, 1]
        ys[i] = lax.select(odd == 1, second, first)
        y_copy(i).start()

    cands = []
    rank = 0
    for i in range(4):
        for from_y in ((True,) if i == 0 else (False, True)):
            group = place(i) * 2 + ((1 - y) if from_y else y)
            even, odd = count(mine, 2 * group), count(mine, 2 * group + 1)
            cands.append((i, from_y, even, odd, rank))
            rank = rank + even + odd

    def slot_stage(k):
        value = None
        for j in range(k, k + 3):
            i, from_y, even, odd, place_of = cands[j]
            if from_y:
                options = [(even + odd, yr[i])]
            else:
                options = [(even, zb[i - 1, 0]), (odd, zb[i - 1, 1])]
            for listed, tile in options:
                if value is None:
                    value = tile
                else:
                    here = jnp.where(place_of == k, listed, 0)
                    value = lax.select(here == 1, tile, value)
        gat[tp, 2 + k] = value
        x_copy(2 + k).start()
        c_copy(2 + k).start()

    def normalize(k, row):
        blocks = [gat[t, k].astype(F32) for t in range(4)]
        width = 4 * cols
        mean = sum(jnp.sum(b, axis=1, keepdims=True) for b in blocks) / width
        blocks = [b - mean for b in blocks]
        var = sum(jnp.sum(b * b, axis=1, keepdims=True) for b in blocks) / width
        scale = lax.rsqrt(var + 1e-06)
        for t in range(4):
            lanes = slice(t * cols, (t + 1) * cols)
            nb[row : row + TILE, lanes] = (
                blocks[t] * scale * (1.0 + mod[1:2, lanes]) + mod[0:1, lanes]
            ).astype(BF16)

    heads = cols // HD
    factor = 1.0 / math.sqrt(HD)

    def project(first, rows):
        normed = nb[0:rows]
        at = first * TILE
        kb[at : at + rows] = jnp.dot(normed, wk[...], preferred_element_type=F32).astype(BF16)
        for h in range(heads):
            lanes = slice(h * HD, (h + 1) * HD)
            sc[h, :, at : at + rows] = (
                lax.dot_general(
                    qb[:, lanes], kb[at : at + rows, lanes], (((1,), (1,)), ((), ())),
                    preferred_element_type=F32,
                )
                * factor
            )
        vb[at : at + rows] = jnp.dot(normed, wv[...], preferred_element_type=F32).astype(BF16)

    def attend(k):
        rest_arrive(k)
        normalize(k, 0)
        project(k, TILE)

    def y_arrive(i):
        y_copy(i).wait_recv()

    outer = zz == 0

    y_stage(0)
    for t in range(2):
        z_arrive(0, t)
        gat[tp, t] = x_ref[t * TILE : (t + 1) * TILE]
        x_arrive(t)

        @pl.when(inner)
        def _():
            z_arrive(1, t)

    y_stage(1)

    @pl.when(inner)
    def _():
        y_stage(2)

    loads[6].wait()
    for t in range(2):
        rest_arrive(t)
        normalize(t, t * TILE)
    for cpy in loads[:3]:
        cpy.wait()
    qb[...] = jnp.dot(nb[...], wq[...], preferred_element_type=F32).astype(BF16)
    project(0, 2 * TILE)

    @pl.when(inner)
    def _():
        z_arrive(2, 0)
        z_arrive(2, 1)
        y_stage(3)

    @pl.when(outer)
    def _():
        z_arrive(1, 0)
        z_arrive(1, 1)
        y_stage(2)

    y_arrive(0)
    y_arrive(1)
    slot_stage(0)
    slot_stage(1)

    @pl.when(outer)
    def _():
        z_arrive(2, 0)

    x_arrive(2)
    y_arrive(2)
    slot_stage(2)

    @pl.when(outer)
    def _():
        z_arrive(2, 1)
        y_stage(3)

    slot_stage(3)
    x_arrive(3)
    attend(2)
    attend(3)
    y_arrive(3)
    slot_stage(4)
    x_arrive(4)
    attend(4)
    x_arrive(5)
    attend(5)

    early = (lists - 1) * TILE
    parts = []
    for h in range(heads):
        lanes = slice(h * HD, (h + 1) * HD)
        scores = sc[h, :, 0:early]
        top = jnp.max(scores, axis=1, keepdims=True)
        full = jnp.exp(scores - top)
        total = jnp.sum(full, axis=1, keepdims=True)
        summed = jnp.dot(full.astype(BF16), vb[0:early, lanes], preferred_element_type=F32)
        acc_ref[h] = summed
        parts.append((top, total))
    x_arrive(6)
    attend(6)

    def att_part(t, h):
        return att.at[t, :, pl.ds(h * HD, HD)]

    def ax_copy(h):
        return remote(att_part(tp, h), att_part(tp, h), axs.at[h], axr.at[h], xp)

    def ac_copy(h):
        return remote(att_part(tp, h), att_part(tp, h), acs.at[h], acr.at[h], cp)

    def ad_copy(h):
        return remote(att_part(tx, h), att_part(tx, h), ads.at[h], adr.at[h], cp)

    for h in range(heads):
        lanes = slice(h * HD, (h + 1) * HD)
        scores = sc[h, :, early:]
        top, total = parts[h]
        row_max = jnp.maximum(top, jnp.max(scores, axis=1, keepdims=True))
        scale = jnp.exp(top - row_max)
        full = jnp.exp(scores - row_max)
        total = total * scale + jnp.sum(full, axis=1, keepdims=True)
        summed = acc_ref[h] * scale + jnp.dot(
            full.astype(BF16), vb[early:, lanes], preferred_element_type=F32
        )
        att[tp, :, lanes] = (summed / total).astype(BF16)
        ax_copy(h).start()
        ac_copy(h).start()

    loads[3].wait()
    acc = jnp.dot(att[tp], wo[tp], preferred_element_type=F32)
    for h in range(heads):
        remote(att_part(tx, h), att_part(tx, h), axs.at[h], axr.at[h], xp).wait_recv()
        ad_copy(h).start()
    for h in range(heads):
        remote(att_part(tc, h), att_part(tc, h), acs.at[h], acr.at[h], cp).wait_recv()
    acc = acc + jnp.dot(att[tc], wo[tc], preferred_element_type=F32)
    acc = acc + jnp.dot(att[tx], wo[tx], preferred_element_type=F32)
    for h in range(heads):
        remote(att_part(td, h), att_part(td, h), ads.at[h], adr.at[h], cp).wait_recv()
    acc = acc + jnp.dot(att[td], wo[td], preferred_element_type=F32)
    gate = mod[2:3, pl.ds(pl.multiple_of(tp * cols, HD), cols)]
    o_ref[...] = (x_ref[...].astype(F32) + gate * acc).astype(BF16)

    for t in range(2):
        z_own_up(t).wait_send()

        @pl.when(inner)
        def _():
            z_own_down(t).wait_send()
            for i in range(3):
                z_forward(i, t).wait_send()

    for i in range(4):
        y_copy(i).wait_send()
    for k in range(lists):
        x_copy(k).wait_send()
        c_copy(k).wait_send()
        d_copy(k).wait_send()
    for h in range(heads):
        ax_copy(h).wait_send()
        ac_copy(h).wait_send()
        ad_copy(h).wait_send()


def fused(states, modulation, query_weight, key_weight, value_weight, out_weight, pattern):
    rows, cols = states.shape
    width = modulation.shape[1]
    lists = pattern.shape[1]
    heads = cols // HD
    vmem = pl.BlockSpec(memory_space=pltpu.VMEM)
    hbm = pl.BlockSpec(memory_space=pltpu.HBM)
    dma = pltpu.SemaphoreType.DMA
    return pl.pallas_call(
        fused_kernel,
        out_shape=jax.ShapeDtypeStruct((rows, cols), BF16),
        in_specs=[hbm] * 7,
        out_specs=vmem,
        scratch_shapes=[
            pltpu.VMEM((3, 2, TILE, cols), BF16),
            pltpu.VMEM((4, TILE, cols), BF16),
            pltpu.VMEM((4, TILE, cols), BF16),
            pltpu.VMEM((4, lists, TILE, cols), BF16),
            pltpu.VMEM((4, rows, cols), BF16),
            pltpu.VMEM((width, cols), BF16),
            pltpu.VMEM((width, cols), BF16),
            pltpu.VMEM((width, cols), BF16),
            pltpu.VMEM((4, cols, cols), BF16),
            pltpu.VMEM((rows, width), BF16),
            pltpu.VMEM((rows, cols), BF16),
            pltpu.VMEM((lists * TILE, cols), BF16),
            pltpu.VMEM((lists * TILE, cols), BF16),
            pltpu.VMEM((heads, rows, lists * TILE), F32),
            pltpu.VMEM((heads, rows, HD), F32),
            pltpu.SMEM(pattern.shape[::-1], jnp.int32),
            pltpu.VMEM((rows, cols), BF16),
            pltpu.VMEM(modulation.shape, F32),
            dma((7,)),
            dma((2,)), dma((2,)), dma((6,)), dma((6,)),
            dma((4,)), dma((4,)),
            dma((lists,)), dma((lists,)), dma((lists,)), dma((lists,)), dma((lists,)), dma((lists,)),
            dma((heads,)), dma((heads,)), dma((heads,)), dma((heads,)), dma((heads,)), dma((heads,)),
        ],
        compiler_params=pltpu.CompilerParams(
            collective_id=0, has_side_effects=True, vmem_limit_bytes=60 * 1024 * 1024
        ),
    )(
        pattern.T, states, modulation, query_weight, key_weight, value_weight,
        out_weight.reshape(4, cols, cols),
    )


def local(states, modulation, query_weight, key_weight, value_weight, out_weight, pattern):
    tok_rows, local_cols = states.shape
    col_start = lax.axis_index("tp") * local_cols
    mod_cols = lax.dynamic_slice_in_dim(modulation, col_start, local_cols, 1)
    states_f = states.astype(jnp.float32)
    gathered = lax.all_gather(states, "tp", axis=1, tiled=True)
    gathered_f = gathered.astype(jnp.float32)
    row_mean = jnp.mean(gathered_f, axis=1, keepdims=True)
    centered = gathered_f - row_mean
    variance = jnp.mean(centered * centered, axis=1, keepdims=True)
    normed = (
        centered * lax.rsqrt(variance + 1e-06) * (1.0 + modulation[1]) + modulation[0]
    ).astype(jnp.bfloat16)
    query = jnp.dot(normed, query_weight, preferred_element_type=jnp.float32).astype(jnp.bfloat16)
    keys = jnp.dot(normed, key_weight, preferred_element_type=jnp.float32).astype(jnp.bfloat16)
    values = jnp.dot(normed, value_weight, preferred_element_type=jnp.float32).astype(jnp.bfloat16)
    head_cols = query.shape[1]
    heads_local = head_cols // HD
    key_value = jnp.concatenate([keys, values], axis=1)
    tiles_dev = tok_rows // TILE
    devices = lax.axis_size("seq")
    seq_index = lax.axis_index("seq")
    list_count = pattern.shape[1]
    groups = pattern.reshape(devices, tiles_dev, list_count)
    first_lists = groups[:, 0, :]
    my_list = lax.dynamic_index_in_dim(first_lists, seq_index, 0, keepdims=False)
    all_tiles = lax.all_gather(key_value, "seq", axis=0, tiled=True)
    tile_store = all_tiles.reshape(devices * tiles_dev, TILE, 2 * head_cols)
    listed_rows = jnp.take(tile_store, my_list, axis=0).reshape(
        list_count * TILE, 2, heads_local, HD
    )
    key_rows = listed_rows[:, 0]
    value_rows = listed_rows[:, 1]
    factor = 1.0 / math.sqrt(HD)
    block_rows = min(512, tok_rows)
    block_count = tok_rows // block_rows

    def attend(query_block):
        scores = (
            jnp.einsum("qhd,khd->hqk", query_block, key_rows, preferred_element_type=jnp.float32)
            * factor
        )
        row_max = jnp.max(scores, axis=2, keepdims=True)
        weights_full = jnp.exp(scores - row_max)
        weight_sum = jnp.sum(weights_full, axis=2)
        weights = weights_full.astype(jnp.bfloat16)
        summed = jnp.einsum("hqk,khd->qhd", weights, value_rows, preferred_element_type=jnp.float32)
        return (summed / jnp.transpose(weight_sum)[:, :, None]).astype(jnp.bfloat16)

    query_blocks = query.reshape(block_count, block_rows, heads_local, HD)
    attended = lax.map(attend, query_blocks).reshape(tok_rows, head_cols)
    projected = jnp.dot(
        lax.all_gather(attended, "tp", axis=1, tiled=True),
        out_weight,
        preferred_element_type=jnp.float32,
    )
    return (states_f + mod_cols[2] * projected).astype(jnp.bfloat16)


def solution(mesh):
    placed = (P("seq", "tp"), P(), P(None, "tp"), P(None, "tp"), P(None, "tp"), P(None, "tp"), P())
    small = mesh.shape["seq"] == 8 and mesh.shape["tp"] == 4
    return jax.shard_map(
        fused if small else local, mesh=mesh, in_specs=placed, out_specs=P("seq", "tp"), check_vma=False
    )
```
